32 devices in a mesh: grp: 2 (over x), chan: 16 (over z, y, core).
Axes of the slice: x: 2, y: 2, z: 4, core: 2. Of those that a mesh axis runs over, the one named last changes fastest.
Arguments:
- voltages: bfloat16 [64, 1024, 1024], P(('grp', 'chan')), parts along dimension 0, may hold values from -6 to 6
- filter_taps: float32 [8, 1024], replicated, may hold values from -2 to 2
- feed_map: int32 [1024], replicated, may hold values from 0 to 1023, each once
- delays: int32 [1024], replicated, may hold values from 0 to 1023
- positions: float32 [2, 1024], replicated, may hold values from -64 to 64
- directions: float32 [2, 64], replicated, may hold values from -1 to 1
- pointing: int32 [256], replicated, may hold values from 0 to 63
Outputs:
- visibility: bfloat16 [32, 2, 1024, 1024], P(('grp', 'chan')), parts along dimension 0
- beams: bfloat16 [32, 2, 256, 32], P(('grp', 'chan')), parts along dimension 0
The draws below stay inside these ranges and needn't reach their ends.
There are 2 independent parts, one for each index of `grp`. The reference program is written for one: setup_inputs(seed, part) draws one part's arguments, and reference() takes and returns one part's arrays. A program takes and returns all parts, laid end to end along the dimension named above; an argument that names none is the same for every part. Nothing has to cross between parts.
Inputs may be any that keep to these rules, and one draw needn't show every extreme that they name: `feed_map`: each feed is named by exactly one input.
All inputs are finite; a program needn't handle non-finite values.
Results may differ from the reference program's by a relative error of at most 0.0074.
Values may be sent and summed in bfloat16 or wider, within the bound.
No kernel may reach another device: no remote copies, remote signals or barrier semaphores. Data moves between devices by JAX's collectives and lax.ppermute only.
A program may use at most 64 MiB of HBM per device.

```python
import math
import jax
import jax.numpy as jnp
from jax import lax

A = 1024
NFFT = 1024
TAPS = 8
BEAMS = 256
DIRS = 64
FRAMES = 32
CHANNELS = 16


def touch_ends(array, own_key, smallest, high):
    longest = array.shape.index(max(array.shape))
    spots = []
    for shift in (0, 1):
        where = [jax.random.randint(jax.random.fold_in(own_key, axis), (), 0, length) for axis, length in enumerate(array.shape)]
        where[longest] = (where[longest] + shift) % array.shape[longest]
        spots.append(tuple(where))
    return array.at[spots[0]].set(smallest).at[spots[1]].set(high)


def levels(rng, shape, cuts, least, top_value):
    level, own = 1.0, jax.random.fold_in(rng, 6)
    for position, parts in cuts:
        heights = jnp.exp(jax.random.uniform(jax.random.fold_in(own, position), (parts,), jnp.float32, least / len(cuts), top_value / len(cuts)))
        level = level * jnp.repeat(heights, shape[position] // parts).reshape([-1 if axis == position else 1 for axis in range(len(shape))])
    return level


def gaussian(own_key, shape, spread, bound, split=(), kind=jnp.bfloat16):
    drawn = spread * jax.random.normal(own_key, shape, jnp.float32)
    if split:
        drawn = drawn * levels(own_key, shape, split, -0.22, 0.18)
    return jnp.clip(drawn, -bound, bound).astype(kind)


def setup_inputs(seed: int = 0, part: int = 0) -> dict:
    key_of = jax.random.split(jax.random.key(seed), 8)
    own_keys = jax.random.split(jax.random.fold_in(key_of[7], part), 8)
    voltages = gaussian(own_keys[0], (FRAMES, NFFT, A), 1.0, 6.0, ((0, 16),))
    filter_taps = gaussian(key_of[1], (TAPS, NFFT), TAPS ** -0.5, 2.0, (), jnp.float32)
    feed_map = jax.random.permutation(key_of[2], A).astype(jnp.int32)
    delays = touch_ends(jax.random.randint(key_of[3], (A,), 0, NFFT), jax.random.fold_in(key_of[3], 1), 0, NFFT - 1).astype(jnp.int32)
    positions = jnp.clip(jax.random.uniform(key_of[4], (2, A), jnp.float32, -64.0, 64.0), -64.0, 64.0)
    directions = jnp.clip(jax.random.uniform(key_of[5], (2, DIRS), jnp.float32, -1.0, 1.0), -1.0, 1.0)
    pointing = touch_ends(jax.random.randint(key_of[6], (BEAMS,), 0, DIRS), jax.random.fold_in(key_of[6], 1), 0, DIRS - 1).astype(jnp.int32)
    return dict(voltages=voltages, filter_taps=filter_taps, feed_map=feed_map, delays=delays, positions=positions, directions=directions, pointing=pointing)


def tapped_table(filter_taps, first_bin, count, length):
    rows_index = (first_bin + jnp.arange(count, dtype=jnp.int32))[:, None]
    cols_index = jnp.arange(length, dtype=jnp.int32)[None, :]
    angles = 2.0 * math.pi / length * (rows_index * cols_index % length).astype(jnp.float32)
    factor = 1.0 / math.sqrt(length)
    base = jnp.concatenate([jnp.cos(angles) * factor, -jnp.sin(angles) * factor], 0)
    return (base[None, :, :] * filter_taps[:, None, :]).astype(jnp.bfloat16)

def reference(voltages, filter_taps, feed_map, delays, positions, directions, pointing):
    extended = jnp.concatenate([jnp.zeros((TAPS - 1, NFFT, A), voltages.dtype), voltages], 0)
    first_bin = NFFT // 2 - CHANNELS
    table = tapped_table(filter_taps, first_bin, CHANNELS, NFFT)
    flat_table = jnp.transpose(table[::-1], (1, 0, 2)).reshape(2 * CHANNELS, TAPS * NFFT)

    def transform(frame_index):
        window = lax.dynamic_slice_in_dim(extended, frame_index, TAPS, 0).reshape(TAPS * NFFT, A)
        result = jnp.dot(flat_table, window, preferred_element_type=jnp.float32).astype(jnp.bfloat16)
        return result.reshape(2, CHANNELS, A)
    spectra = lax.map(transform, jnp.arange(FRAMES, dtype=jnp.int32))
    by_channel = jnp.moveaxis(spectra, 2, 0)
    one_hot = (pointing[:, None] == jnp.arange(DIRS, dtype=jnp.int32)[None, :]).astype(jnp.float32)
    east = lax.optimization_barrier(jnp.sum(one_hot * directions[0][None, :], axis=1))
    north = lax.optimization_barrier(jnp.sum(one_hot * directions[1][None, :], axis=1))
    geo_delay = east[:, None] * positions[0][None, :] + north[:, None] * positions[1][None, :]

    def channel_work(operands):
        block, bin_value = operands
        mapped = block[:, :, feed_map].astype(jnp.float32)
        phases = 2.0 * math.pi / NFFT * (bin_value * delays % NFFT).astype(jnp.float32)
        cosine = jnp.cos(phases)
        sine = jnp.sin(phases)
        real_part = (mapped[:, 0] * cosine + mapped[:, 1] * sine).astype(jnp.bfloat16)
        imag_part = (mapped[:, 1] * cosine - mapped[:, 0] * sine).astype(jnp.bfloat16)
        stacked = jnp.concatenate([real_part, imag_part], 0)
        rotated = jnp.concatenate([imag_part, -real_part], 0)
        vis_real = jnp.dot(stacked.T, stacked, preferred_element_type=jnp.float32)
        vis_imag = jnp.dot(rotated.T, stacked, preferred_element_type=jnp.float32)
        visibility = (jnp.stack([vis_real, vis_imag]) * (1.0 / FRAMES)).astype(jnp.bfloat16)
        fraction = geo_delay * (bin_value.astype(jnp.float32) / NFFT)
        angles = 2.0 * math.pi * (fraction - jnp.floor(fraction))
        wave_cos = jnp.cos(angles).astype(jnp.bfloat16)
        wave_sin = jnp.sin(angles).astype(jnp.bfloat16)
        voices = jnp.concatenate([real_part, imag_part], 1)
        beam_real = jnp.dot(jnp.concatenate([wave_cos, wave_sin], 1), voices.T, preferred_element_type=jnp.float32)
        beam_imag = jnp.dot(jnp.concatenate([-wave_sin, wave_cos], 1), voices.T, preferred_element_type=jnp.float32)
        beams = (jnp.stack([beam_real, beam_imag]) * (1.0 / math.sqrt(A))).astype(jnp.bfloat16)
        return (visibility, beams)
    bin_values = first_bin + jnp.arange(CHANNELS, dtype=jnp.int32)
    visibility, beams = lax.map(channel_work, (by_channel, bin_values))
    return (visibility, beams)
```

```python
import functools
import math

import jax
import jax.numpy as jnp
from jax import lax
from jax.experimental import pallas as pl
from jax.experimental.pallas import tpu as pltpu
from jax.sharding import PartitionSpec as P


F32 = jnp.float32
BF16 = jnp.bfloat16
I32 = jnp.int32
VMEM = pltpu.VMEM


def iota(shape, dim):
    return lax.broadcasted_iota(I32, shape, dim)


def relative_channel(index, quarter):
    group = index // quarter
    low = jnp.where(group == 0, 3, jnp.where(group == 1, 1, jnp.where(group == 2, 2, 0)))
    return low + 4 * (index % quarter)


def filter_kernel(channels, blocks, taps_hbm, volt_hbm, send_ref, keep_ref, taps, volt, table, sems):
    tap_count, length = taps.shape
    frames, _, inputs = volt.shape
    rows = 2 * channels
    half = rows // 2
    width = inputs // blocks
    taps_copy = pltpu.make_async_copy(taps_hbm, taps, sems.at[blocks])
    taps_copy.start()
    copies = []
    for b in range(blocks):
        cut = (slice(None), slice(None), pl.ds(b * width, width))
        copies.append(pltpu.make_async_copy(volt_hbm.at[cut], volt.at[cut], sems.at[b]))
        copies[-1].start()
    me = lax.axis_index("chan")
    row = iota((rows, length), 0)
    channel = me ^ relative_channel(row // 2, channels // 4)
    step = (length // 2 - channels + channel) * iota((rows, length), 1)
    turn = (step + (row % 2) * (length // 4)) % length
    base = jnp.cos((2.0 * math.pi / length) * turn.astype(F32)) * (1.0 / math.sqrt(length))
    taps_copy.wait()
    for t in range(tap_count):
        table[t * rows : (t + 1) * rows, :] = (base * taps[t : t + 1, :]).astype(BF16)
    for b in range(blocks):
        copies[b].wait()
        lanes = slice(b * width, (b + 1) * width)
        terms = [
            jnp.dot(table[...], volt[s, :, lanes], preferred_element_type=F32)
            for s in range(frames)
        ]
        for w in range(frames + tap_count - 1):
            total = None
            for s in range(frames):
                if 0 <= w - s < tap_count:
                    term = terms[s][(w - s) * rows : (w - s + 1) * rows]
                    total = term if total is None else total + term
            send_ref[w, :, lanes] = total[:half].astype(BF16)
            keep_ref[w, :, lanes] = total[half:]


def pair_kernel(frames, bit, own_ref, recv_ref, send_ref, keep_ref):
    window, rows, _ = own_ref.shape
    half = rows // 2
    late = (lax.axis_index("chan") // bit) % 2

    def body(first, second):
        for w in range(window + frames):
            total = None
            if w < window:
                total = first[w].astype(F32)
            if w >= frames:
                term = second[w - frames].astype(F32)
                total = term if total is None else total + term
            send_ref[w * half : (w + 1) * half, :] = total[:half].astype(BF16)
            keep_ref[w * half : (w + 1) * half, :] = total[half:].astype(BF16)

    @pl.when(late == 0)
    def _():
        body(own_ref, recv_ref)

    @pl.when(late == 1)
    def _():
        body(recv_ref, own_ref)


def spread_kernel(frames, bit, planes, own_ref, recv_ref, *outs):
    size = own_ref.shape[0]
    padded = outs[0].shape[0] // 2
    late = (lax.axis_index("chan") // bit) % 2
    shape = (planes * 2 * padded, size)
    out_row = iota(shape, 0)
    in_row = iota(shape, 1)
    same = (out_row // padded) == (in_row % (2 * planes))
    lag = (out_row % padded) - in_row // (2 * planes)
    own_pick = (same & (lag == late * frames)).astype(F32).astype(BF16)
    recv_pick = (same & (lag == (1 - late) * frames)).astype(F32).astype(BF16)
    total = jnp.dot(own_pick, own_ref[...], preferred_element_type=F32)
    total = total + jnp.dot(recv_pick, recv_ref[...], preferred_element_type=F32)
    for k in range(planes):
        outs[k][...] = total[k * 2 * padded : (k + 1) * 2 * padded].astype(BF16)


def final_kernel(planes, plane_frames, total_frames, *refs):
    chunks = refs[:planes]
    order_ref, phase_ref, steer_ref, spread_ref = refs[planes : planes + 4]
    vis_ref, beams_ref, gathered, left = refs[planes + 4 :]
    rows, inputs = chunks[0].shape
    padded = rows // 2
    block = vis_ref.shape[2]
    step = pl.program_id(0)

    @pl.when(step == 0)
    def _():
        for k in range(planes):
            gathered[k * rows : (k + 1) * rows, :] = chunks[k][...]
        plane = lax.axis_index("chan") // 4
        shape = (2 * total_frames, planes * rows)
        out_row = iota(shape, 0)
        in_row = iota(shape, 1)
        start = (plane ^ (in_row // rows)) * plane_frames
        inside = in_row % rows
        same = (out_row // total_frames) == (inside // padded)
        pick = same & ((out_row % total_frames) == start + inside % padded)
        spectra = jnp.dot(pick.astype(F32).astype(BF16), gathered[...], preferred_element_type=F32)
        mapped = jnp.dot(spectra.astype(BF16), order_ref[...], preferred_element_type=F32)
        xr = mapped[:total_frames]
        xi = mapped[total_frames:]
        cosine = phase_ref[0:1, :]
        sine = phase_ref[1:2, :]
        yr = (xr * cosine + xi * sine).astype(BF16)
        yi = (xi * cosine - xr * sine).astype(BF16)
        left[0, :total_frames, :] = yr
        left[0, total_frames:, :] = yi
        left[1, :total_frames, :] = yi
        left[1, total_frames:, :] = -yr
        dirs = steer_ref.shape[0] // 2
        formed = lax.dot_general(
            left[0], steer_ref[...], (((1,), (1,)), ((), ())), preferred_element_type=F32
        )
        rc = formed[:total_frames, :dirs]
        rs = formed[:total_frames, dirs:]
        ic = formed[total_frames:, :dirs]
        iss = formed[total_frames:, dirs:]
        scale = 1.0 / math.sqrt(inputs)
        beams_ref[0] = jnp.dot(
            ((rc + iss) * scale).astype(BF16), spread_ref[...], preferred_element_type=F32
        ).astype(BF16)
        beams_ref[1] = jnp.dot(
            ((ic - rs) * scale).astype(BF16), spread_ref[...], preferred_element_type=F32
        ).astype(BF16)

    lanes = pl.ds(pl.multiple_of(step * block, block), block)
    for q in range(2):
        vis = lax.dot_general(
            left[q, :, lanes], left[0], (((0,), (0,)), ((), ())), preferred_element_type=F32
        )
        vis_ref[0, q] = (vis * (1.0 / total_frames)).astype(BF16)


def params(mib, semantics=None):
    return pltpu.CompilerParams(
        vmem_limit_bytes=mib * 2**20,
        dimension_semantics=semantics,
    )


def cost(flops, moved):
    return pl.CostEstimate(flops=flops, bytes_accessed=moved, transcendentals=0)


def local(voltages, filter_taps, feed_map, delays, positions, directions, pointing):
    tap_count, length = filter_taps.shape
    frames, _, inputs = voltages.shape
    devices = lax.axis_size("chan")
    if devices < 4 or devices & (devices - 1):
        raise ValueError("chan size")
    total_frames = frames * devices
    planes = devices // 4
    first_bin = length // 2 - devices
    me = lax.axis_index("chan")
    window = frames + tap_count - 1
    any_spec = pl.BlockSpec(memory_space=pltpu.HBM)
    vmem_spec = pl.BlockSpec(memory_space=VMEM)

    blocks = 4
    send, keep = pl.pallas_call(
        functools.partial(filter_kernel, devices, blocks),
        out_shape=(
            jax.ShapeDtypeStruct((window, devices, inputs), BF16),
            jax.ShapeDtypeStruct((window, devices, inputs), F32),
        ),
        in_specs=[any_spec, any_spec],
        out_specs=(vmem_spec, vmem_spec),
        scratch_shapes=[
            VMEM((tap_count, length), F32),
            VMEM((frames, length, inputs), BF16),
            VMEM((tap_count * 2 * devices, length), BF16),
            pltpu.SemaphoreType.DMA((blocks + 1,)),
        ],
        compiler_params=params(24),
        cost_estimate=cost(
            4 * frames * length * inputs * devices * tap_count, 2 * frames * length * inputs
        ),
        name="filter",
    )(pltpu.with_memory_space_constraint(filter_taps, pltpu.HBM), pltpu.with_memory_space_constraint(voltages, pltpu.HBM))

    def swap(value, bits):
        return lax.ppermute(value, "chan", [(i, i ^ bits) for i in range(devices)])

    recv = swap(send, 1)
    wide = window + frames
    shape = jax.ShapeDtypeStruct((wide * devices // 2, inputs), BF16)
    send, keep = pl.pallas_call(
        functools.partial(pair_kernel, frames, 1),
        out_shape=(shape, shape),
        in_specs=[vmem_spec, vmem_spec],
        out_specs=(vmem_spec, vmem_spec),
        compiler_params=params(16),
        cost_estimate=cost(0, 8 * window * devices * inputs),
        name="pair",
    )(keep, recv)

    send, feed_map, delays, positions, directions, pointing = lax.optimization_barrier(
        (send, feed_map, delays, positions, directions, pointing)
    )
    recv = swap(send, 2)
    padded = -(-(window + 3 * frames) // 16) * 16
    shape = jax.ShapeDtypeStruct((2 * padded, inputs), BF16)
    outs = pl.pallas_call(
        functools.partial(spread_kernel, 2 * frames, 2, planes),
        out_shape=(shape,) * planes,
        in_specs=[vmem_spec, vmem_spec],
        out_specs=(vmem_spec,) * planes,
        compiler_params=params(16),
        cost_estimate=cost(0, 8 * wide * devices * inputs),
        name="spread",
    )(keep, recv)

    chunks = [outs[0]] + [swap(outs[k], 4 * k) for k in range(1, planes)]

    order = (feed_map[None, :] == jnp.arange(inputs, dtype=I32)[:, None]).astype(BF16)
    local_bin = first_bin + me
    phases = 2.0 * math.pi / length * (local_bin * delays % length).astype(F32)
    phase = jnp.stack([jnp.cos(phases), jnp.sin(phases)], 0)
    geo = (
        directions[0][:, None] * positions[0][None, :]
        + directions[1][:, None] * positions[1][None, :]
    )
    fraction = geo * (local_bin.astype(F32) / length)
    angles = 2.0 * math.pi * (fraction - jnp.floor(fraction))
    steer = jnp.concatenate([jnp.cos(angles), jnp.sin(angles)], 0).astype(BF16)
    table_size = directions.shape[1]
    spread = (jnp.arange(table_size, dtype=I32)[:, None] == pointing[None, :]).astype(BF16)

    beams_count = pointing.shape[0]
    block = min(256, inputs)

    def whole(shape):
        return pl.BlockSpec(shape, lambda i: (0,) * len(shape))

    visibility, beams = pl.pallas_call(
        functools.partial(final_kernel, planes, 4 * frames, total_frames),
        out_shape=(
            jax.ShapeDtypeStruct((1, 2, inputs, inputs), BF16),
            jax.ShapeDtypeStruct((2, total_frames, beams_count), BF16),
        ),
        grid=(inputs // block,),
        in_specs=[whole((2 * padded, inputs))] * planes
        + [whole(order.shape), whole(phase.shape), whole(steer.shape), whole(spread.shape)],
        out_specs=(
            pl.BlockSpec((1, 2, block, inputs), lambda i: (0, 0, i, 0)),
            whole((2, total_frames, beams_count)),
        ),
        scratch_shapes=[
            VMEM((planes * 2 * padded, inputs), BF16),
            VMEM((2, 2 * total_frames, inputs), BF16),
        ],
        compiler_params=params(24, ("arbitrary",)),
        cost_estimate=cost(8 * total_frames * inputs * inputs, 4 * inputs * inputs),
        name="final",
    )(*chunks, order, phase, steer, spread)
    return (visibility, jnp.swapaxes(beams, 1, 2)[None])


def solution(mesh):
    in_specs = (P(("grp", "chan"), None, None), P(), P(), P(), P(), P(), P())
    out_specs = (P(("grp", "chan"), None, None, None), P(("grp", "chan"), None, None, None))
    return jax.shard_map(local, mesh=mesh, in_specs=in_specs, out_specs=out_specs, check_vma=False)
```

```python
import functools
import math

import jax
import jax.numpy as jnp
from jax import lax
from jax.experimental import pallas as pl
from jax.experimental.pallas import tpu as pltpu
from jax.sharding import PartitionSpec as P


F32 = jnp.float32
BF16 = jnp.bfloat16
I32 = jnp.int32
VMEM = pltpu.VMEM
MIB = 2**20


def iota(shape, dim):
    return lax.broadcasted_iota(I32, shape, dim)


def routes(chips):
    measured = {8: ((7, 3, 1, 0), (5, 4, 2, 6))}
    half = chips // 2
    return measured.get(chips, (tuple(range(half))[::-1], tuple(range(half, chips))))


def distance(route, side, index):
    value = jnp.zeros_like(index)
    for k in range(len(route[0])):
        value = jnp.where(index == k, jnp.where(side == 0, route[0][k], route[1][k]), value)
    return value


def wrap(value, length):
    return value & (length - 1) if length & (length - 1) == 0 else value % length


def filter_kernel(channels, route, taps_hbm, volt_hbm, send_ref, keep_ref, taps, volt, table, acc, sems):
    tap_count, length = taps.shape
    frames, _, inputs = volt.shape
    rows = 2 * channels
    half = rows // 2
    blocks = sems.shape[0] - 1
    depth = length // blocks
    taps_copy = pltpu.make_async_copy(taps_hbm, taps, sems.at[blocks])
    taps_copy.start()
    copies = []
    for b in range(blocks):
        cut = (slice(None), pl.ds(b * depth, depth), slice(None))
        copies.append(pltpu.make_async_copy(volt_hbm.at[cut], volt.at[cut], sems.at[b]))
        copies[-1].start()
    me = lax.axis_index("chan")
    core = me % 2
    row = iota((rows, 1), 0)
    side = jnp.where(row < half, 1 - core, core)
    chip = (me // 2) ^ distance(route, side, (row % half) // 4)
    bins = length // 2 - channels + 2 * chip + (row // 2) % 2
    turn = wrap(bins * iota((rows, length), 1) + (row % 2) * (length // 4), length)
    base = jnp.cos((2.0 * math.pi / length) * turn.astype(F32)) * (1.0 / math.sqrt(length))
    taps_copy.wait()
    for t in range(tap_count):
        table[t * rows : (t + 1) * rows, :] = (base * taps[t : t + 1, :]).astype(BF16)
    for b in range(blocks):
        copies[b].wait()
        cut = slice(b * depth, (b + 1) * depth)
        for s in range(frames):
            term = jnp.dot(table[:, cut], volt[s, cut, :], preferred_element_type=F32)
            if b == 0:
                acc[s] = term
            else:
                acc[s] += term
    for w in range(frames + tap_count - 1):
        total = None
        for s in range(frames):
            if 0 <= w - s < tap_count:
                term = acc[s, (w - s) * rows : (w - s + 1) * rows, :]
                total = term if total is None else total + term
        send_ref[w * half : (w + 1) * half, :] = total[:half].astype(BF16)
        keep_ref[w * half : (w + 1) * half, :] = total[half:].astype(BF16)


def pair_kernel(frames, own_ref, recv_ref, *outs):
    size = own_ref.shape[0]
    count = len(outs)
    rows = outs[0].shape[0]
    padded = rows // 4
    core = lax.axis_index("chan") % 2
    shape = (count * rows, size)
    out_row = iota(shape, 0)
    in_row = iota(shape, 1)
    same = (out_row // padded) == (in_row % (4 * count))
    lag = (out_row % padded) - in_row // (4 * count)
    own_pick = (same & (lag == core * frames)).astype(F32).astype(BF16)
    recv_pick = (same & (lag == (1 - core) * frames)).astype(F32).astype(BF16)
    total = jnp.dot(own_pick, own_ref[...], preferred_element_type=F32)
    total = total + jnp.dot(recv_pick, recv_ref[...], preferred_element_type=F32)
    for k in range(count):
        outs[k][...] = total[k * rows : (k + 1) * rows].astype(BF16)


def gather_kernel(route, chip_frames, *refs):
    count = len(route[0])
    chunks = refs[:count]
    send_ref, keep_ref, gathered = refs[count:]
    rows = chunks[0].shape[0]
    padded = rows // 4
    total_frames = send_ref.shape[0] // 2
    me = lax.axis_index("chan")
    core = me % 2
    for k in range(count):
        gathered[k * rows : (k + 1) * rows, :] = chunks[k][...]
    shape = (4 * total_frames, count * rows)
    out_row = iota((4 * total_frames, 1), 0)
    in_row = iota((1, count * rows), 1)
    out_core = jnp.where(out_row < 2 * total_frames, 1 - core, core)
    out_key = (out_core * 2 + (out_row // total_frames) % 2) * total_frames + out_row % total_frames
    chip = (me // 2) ^ distance(route, core, in_row // rows)
    frame = chip * chip_frames + in_row % padded
    in_key = ((in_row % rows) // padded) * total_frames + frame
    in_key = jnp.where(frame < total_frames, in_key, -1)
    pick = jnp.broadcast_to(out_key, shape) == jnp.broadcast_to(in_key, shape)
    total = jnp.dot(pick.astype(F32).astype(BF16), gathered[...], preferred_element_type=F32)
    send_ref[...] = total[: 2 * total_frames].astype(send_ref.dtype)
    keep_ref[...] = total[2 * total_frames :]


def final_kernel(blocks, own_ref, recv_ref, order_ref, phase_ref, steer_ref, spread_ref, vis_hbm, beams_hbm, left, vis, formed, sems):
    inputs = own_ref.shape[1]
    total_frames = own_ref.shape[0] // 2
    block = inputs // blocks
    spectra = (own_ref[...] + recv_ref[...].astype(F32)).astype(BF16)
    mapped = jnp.dot(spectra, order_ref[...], preferred_element_type=F32)
    xr = mapped[:total_frames]
    xi = mapped[total_frames:]
    cosine = phase_ref[0:1, :]
    sine = phase_ref[1:2, :]
    yr = (xr * cosine + xi * sine).astype(BF16)
    yi = (xi * cosine - xr * sine).astype(BF16)
    left[0, :total_frames, :] = yr
    left[0, total_frames:, :] = yi
    left[1, :total_frames, :] = yi
    left[1, total_frames:, :] = -yr
    copies = []
    for b in range(blocks):
        cut = slice(b * block, (b + 1) * block)
        for q in range(2):
            value = lax.dot_general(
                left[q, :, cut], left[0], (((0,), (0,)), ((), ())), preferred_element_type=F32
            )
            vis[q, cut, :] = (value * (1.0 / total_frames)).astype(BF16)
        rows = pl.ds(b * block, block)
        copies.append(pltpu.make_async_copy(vis.at[:, rows], vis_hbm.at[0, :, rows], sems.at[b]))
        copies[-1].start()
        if b == blocks // 2:
            dirs = steer_ref.shape[0] // 2
            terms = lax.dot_general(
                left[0], steer_ref[...], (((1,), (1,)), ((), ())), preferred_element_type=F32
            )
            real = terms[:total_frames, :dirs] + terms[total_frames:, dirs:]
            imag = terms[total_frames:, :dirs] - terms[:total_frames, dirs:]
            scale = 1.0 / math.sqrt(inputs)
            for q, value in enumerate((real, imag)):
                formed[q] = jnp.dot(
                    (value * scale).astype(BF16), spread_ref[...], preferred_element_type=F32
                ).astype(BF16)
            copies.append(pltpu.make_async_copy(formed, beams_hbm, sems.at[blocks]))
            copies[-1].start()
    for copy in copies:
        copy.wait()


def params(need):
    return pltpu.CompilerParams(vmem_limit_bytes=min(int(1.5 * need) + 8 * MIB, 60 * MIB))


def cost(flops, moved):
    return pl.CostEstimate(flops=flops, bytes_accessed=moved, transcendentals=0)


def in_hbm(value):
    return pltpu.with_memory_space_constraint(value, pltpu.HBM)


def local(voltages, filter_taps, feed_map, delays, positions, directions, pointing):
    tap_count, length = filter_taps.shape
    frames, _, inputs = voltages.shape
    devices = lax.axis_size("chan")
    if devices < 4 or devices & (devices - 1):
        raise ValueError("chan size")
    total_frames = frames * devices
    chips = devices // 2
    route = routes(chips)
    count = chips // 2
    first_bin = length // 2 - devices
    me = lax.axis_index("chan")
    window = frames + tap_count - 1
    hbm = pl.BlockSpec(memory_space=pltpu.HBM)
    vmem = pl.BlockSpec(memory_space=VMEM)

    blocks = max(length // 256, 1)
    table_rows = tap_count * 2 * devices
    shape = jax.ShapeDtypeStruct((window * devices, inputs), BF16)
    send, keep = pl.pallas_call(
        functools.partial(filter_kernel, devices, route),
        out_shape=(shape, shape),
        in_specs=[hbm, hbm],
        out_specs=(vmem, vmem),
        scratch_shapes=[
            VMEM((tap_count, length), F32),
            VMEM((frames, length, inputs), BF16),
            VMEM((table_rows, length), BF16),
            VMEM((frames, table_rows, inputs), F32),
            pltpu.SemaphoreType.DMA((blocks + 1,)),
        ],
        compiler_params=params(
            2 * frames * length * inputs + 2 * table_rows * length + 4 * frames * table_rows * inputs
        ),
        cost_estimate=cost(
            2 * frames * length * inputs * table_rows, 2 * frames * length * inputs
        ),
        name="filter",
    )(in_hbm(filter_taps), in_hbm(voltages))

    other_core = [(i, i ^ 1) for i in range(devices)]
    recv = lax.ppermute(send, "chan", other_core)
    padded = -(-(window + frames) // 4) * 4
    shape = jax.ShapeDtypeStruct((4 * padded, inputs), BF16)
    chunks = pl.pallas_call(
        functools.partial(pair_kernel, frames),
        out_shape=(shape,) * count,
        in_specs=[vmem, vmem],
        out_specs=(vmem,) * count,
        compiler_params=params(16 * window * devices * inputs),
        cost_estimate=cost(0, 8 * window * devices * inputs),
        name="pair",
    )(keep, recv)

    *chunks, feed_map, delays, positions, directions, pointing = lax.optimization_barrier(
        (*chunks, feed_map, delays, positions, directions, pointing)
    )
    arrived = []
    for k in range(count):
        pairs = [(i, i ^ (2 * route[i % 2][k])) for i in range(devices)]
        arrived.append(lax.ppermute(chunks[k], "chan", pairs))

    order = (feed_map[None, :] == jnp.arange(inputs, dtype=I32)[:, None]).astype(BF16)
    local_bin = first_bin + me
    phases = 2.0 * math.pi / length * (local_bin * delays % length).astype(F32)
    phase = jnp.stack([jnp.cos(phases), jnp.sin(phases)], 0)
    geo = (
        directions[0][:, None] * positions[0][None, :]
        + directions[1][:, None] * positions[1][None, :]
    )
    fraction = geo * (local_bin.astype(F32) / length)
    angles = 2.0 * math.pi * (fraction - jnp.floor(fraction))
    steer = jnp.concatenate([jnp.cos(angles), jnp.sin(angles)], 0).astype(BF16)
    table_size = directions.shape[1]
    spread = (jnp.arange(table_size, dtype=I32)[:, None] == pointing[None, :]).astype(BF16)

    send, keep = pl.pallas_call(
        functools.partial(gather_kernel, route, 2 * frames),
        out_shape=(
            jax.ShapeDtypeStruct((2 * total_frames, inputs), BF16),
            jax.ShapeDtypeStruct((2 * total_frames, inputs), F32),
        ),
        in_specs=[vmem] * count,
        out_specs=(vmem, vmem),
        scratch_shapes=[VMEM((count * 4 * padded, inputs), BF16)],
        compiler_params=params(16 * count * 4 * padded * inputs),
        cost_estimate=cost(0, 8 * count * padded * inputs),
        name="gather",
    )(*arrived)

    recv = lax.ppermute(send, "chan", other_core)
    beams_count = pointing.shape[0]
    blocks = max(inputs // 128, 1)
    visibility, beams = pl.pallas_call(
        functools.partial(final_kernel, blocks),
        out_shape=(
            jax.ShapeDtypeStruct((1, 2, inputs, inputs), BF16),
            jax.ShapeDtypeStruct((2, total_frames, beams_count), BF16),
        ),
        in_specs=[vmem] * 6,
        out_specs=(hbm, hbm),
        scratch_shapes=[
            VMEM((2, 2 * total_frames, inputs), BF16),
            VMEM((2, inputs, inputs), BF16),
            VMEM((2, total_frames, beams_count), BF16),
            pltpu.SemaphoreType.DMA((blocks + 1,)),
        ],
        compiler_params=params(8 * inputs * inputs + 32 * total_frames * inputs),
        cost_estimate=cost(8 * total_frames * inputs * inputs, 4 * inputs * inputs),
        name="final",
    )(keep, recv, order, phase, steer, spread)
    return (visibility, jnp.swapaxes(beams, 1, 2)[None])


def solution(mesh):
    in_specs = (P(("grp", "chan"), None, None), P(), P(), P(), P(), P(), P())
    out_specs = (P(("grp", "chan"), None, None, None), P(("grp", "chan"), None, None, None))
    return jax.shard_map(local, mesh=mesh, in_specs=in_specs, out_specs=out_specs, check_vma=False)
```
